512 devices in a mesh: dp: 32 (over z, core), expert: 16 (over y, x).
Axes of the slice: x: 4, y: 4, z: 16, core: 2. Of those that a mesh axis runs over, the one named last changes fastest.
Arguments:
- feats: bfloat16 [65536, 1152], P(('dp', 'expert')), may hold values from -6 to 6
- proj: bfloat16 [1152, 1024], replicated, may hold values from -0.1875 to 0.1875
- proj_bias: float32 [1024], replicated, may hold values from -3 to 3
- norm_gain: float32 [1024], replicated, may hold values from 0.1 to 1.9
- expert_ids: int32 [65536, 6], P(('dp', 'expert')), may hold values from 0 to 31, all different within a row; in each aligned block of 128 rows (0 to 127, 128 to 255, ...) at most 25 rows name the same one
- gate_codes: int32 [65536, 6], P(('dp', 'expert')), may hold values from 4 to 64
- w_gate: bfloat16 [32, 1024, 768], P('expert', 'dp'), may hold values from -0.1875 to 0.1875
- w_up: bfloat16 [32, 1024, 768], P('expert', 'dp'), may hold values from -0.1875 to 0.1875
- w_down_t: bfloat16 [32, 1024, 768], P('expert', 'dp'), may hold values from -0.21875 to 0.21875
- out_grad: bfloat16 [65536, 1024], P(('dp', 'expert')), may hold values from -6 to 6
Outputs:
- layer_out: bfloat16 [65536, 1024], P(('dp', 'expert'))
- feat_grad: bfloat16 [65536, 1152], P(('dp', 'expert'))
The draws below stay inside these ranges and needn't reach their ends.
Inputs may be any that keep to these rules, and one draw needn't show every extreme that they name: `expert_ids`: each row names 6 different experts. Among the 128 rows of one device no expert is named by more than 25 rows, and in some device's rows one expert is named by exactly 25.
All inputs are finite; a program needn't handle non-finite values.
Results may differ from the reference program's by a relative error of at most 0.017.
Values may be sent and summed in bfloat16 or wider, within the bound.
No kernel may reach another device: no remote copies, remote signals or barrier semaphores. Data moves between devices by JAX's collectives and lax.ppermute only.
A program may use at most 64 MiB of HBM per device.

```python
import math
import jax
import jax.numpy as jnp
import numpy as np
from jax import lax

FEAT = 1152
D = 1024
FF = 768
EXPERTS = 32
TOP = 6
TOK_DEV = 128
CAP = 25
TOKENS = 65536
N_DP = 32
N_EXPERT = 16


def place_ends(values, stream_key, smallest, top_value):
    longest = values.shape.index(max(values.shape))
    spots = []
    for shift in (0, 1):
        where = [jax.random.randint(jax.random.fold_in(stream_key, axis), (), 0, length) for axis, length in enumerate(values.shape)]
        where[longest] = (where[longest] + shift) % values.shape[longest]
        spots.append(tuple(where))
    return values.at[spots[0]].set(smallest).at[spots[1]].set(top_value)


def levels(own_key, extent, shards, smallest, largest):
    def one(position, parts):
        steps = jax.random.uniform(jax.random.fold_in(jax.random.fold_in(own_key, 6), position), (parts,), jnp.float32, smallest / len(shards), largest / len(shards))
        return jnp.repeat(jnp.exp(steps), extent[position] // parts).reshape((-1,) + (1,) * (len(extent) - position - 1))

    gain = one(*shards[0])
    for cut in shards[1:]:
        gain = gain * one(*cut)
    return gain


def shared_out(rng, own, number, rows, amount, top, limit, skew):
    ranking = jax.random.permutation(rng, amount)
    heavy_load, common = shares(amount, rows * top, limit, skew, True), shares(amount, rows * top, limit, skew, False)
    places = jnp.arange(amount)

    def named(sizes, turn):
        used = int((sizes > 0).sum())
        fixed = max(1, used // 4)
        passed = fixed + (places - fixed + turn * (used - fixed)) % max(1, amount - fixed)
        return jnp.zeros((amount,), jnp.int32).at[ranking[jnp.where(places < fixed, places, passed)]].set(jnp.asarray(sizes, jnp.int32))

    sizes = jnp.where(number % 4 == 0, named(heavy_load, number // 4), named(common, number - number // 4 - 1))
    mixed = jax.random.permutation(jax.random.fold_in(own, 3), amount)
    giver, receiver = mixed[0:amount // 2 * 2:2], mixed[1:amount // 2 * 2:2]
    margin = jnp.minimum(sizes[giver] - 1, limit - sizes[receiver]) // 2
    margin = jnp.where((giver == ranking[0]) | (receiver == ranking[0]) | (sizes[receiver] == 0), 0, jnp.maximum(margin, 0))
    passed = jax.random.randint(jax.random.fold_in(own, 4), (amount // 2,), 0, 1 << 20) % (margin + 1)
    sizes = sizes.at[giver].add(-passed).at[receiver].add(passed)
    labels = jnp.searchsorted(jnp.cumsum(sizes), jnp.arange(rows * top), side="right").astype(jnp.int32)
    listing = labels.reshape(top, rows).T
    listing = listing[jax.random.permutation(jax.random.fold_in(own, 1), rows)]
    turn = jax.random.randint(jax.random.fold_in(own, 2), (rows, 1), 0, top)
    return jnp.take_along_axis(listing, (jnp.arange(top)[None, :] + turn) % top, axis=1)


def shares(number_of, total, reach, skew, full):
    weights = [(1 << 20) // math.isqrt(standing ** skew) + 1 for standing in range(1, number_of + 1)]
    largest = reach if full else min(reach, max(-(-total // number_of), total * weights[0] // sum(weights)))
    least = 1 if total - largest >= number_of - 1 else 0
    given, spare = [largest] + [least] * (number_of - 1), total - largest - least * (number_of - 1)
    while spare > 0:
        free = [i for i in range(1, number_of) if given[i] < largest] or [i for i in range(1, number_of) if given[i] < reach]
        mass, remaining = sum([weights[i] for i in free]), spare
        for i in free:
            extra = min(reach - given[i], max(1, remaining * weights[i] // mass), spare)
            given[i] = given[i] + extra
            spare = spare - extra
    return np.array(given)


def noise(rng, dims, scale, bound, cuts=(), held_as=jnp.bfloat16):
    result = jax.random.normal(rng, dims, jnp.float32) * scale
    if len(cuts) > 0:
        result = levels(rng, dims, cuts, -0.22, 0.18) * result
    return jnp.clip(result, min=-bound, max=bound).astype(held_as)


def setup_inputs(seed: int = 0) -> dict:
    seeds = jax.random.split(jax.random.key(seed), 11)
    feats = noise(seeds[0], (TOKENS, FEAT), 1.0, 6.0, ((0, 512),))
    proj = noise(seeds[1], (FEAT, D), FEAT ** -0.5, 0.1875)
    proj_bias = noise(seeds[2], (D,), 0.5, 3.0, (), jnp.float32)
    norm_gain = jnp.clip(1.0 + 0.18 * jax.random.normal(seeds[3], (D,), jnp.float32), 0.1, 1.9)
    expert_ids_keys = jax.random.split(jax.random.fold_in(seeds[4], 1), TOKENS // TOK_DEV)
    expert_ids_turns = jax.random.permutation(jax.random.fold_in(seeds[4], 3), TOKENS // TOK_DEV)
    expert_ids = jax.vmap(lambda own, number: shared_out(jax.random.fold_in(seeds[4], 2), own, number, TOK_DEV, EXPERTS, TOP, CAP, 1))(expert_ids_keys, expert_ids_turns).reshape((TOKENS, TOP))
    gate_codes = place_ends(jax.random.randint(seeds[5], (TOKENS, TOP), 4, 65), jax.random.fold_in(seeds[5], 1), 4, 64).astype(jnp.int32)
    w_gate = noise(seeds[6], (EXPERTS, D, FF), D ** -0.5, 0.1875, ((0, 16), (1, 32)))
    w_up = noise(seeds[7], (EXPERTS, D, FF), D ** -0.5, 0.1875, ((0, 16), (1, 32)))
    w_down_t = noise(seeds[8], (EXPERTS, D, FF), FF ** -0.5, 0.21875, ((0, 16), (1, 32)))
    out_grad = noise(seeds[9], (TOKENS, D), 1.0, 6.0, ((0, 512),))
    return dict(feats=feats, proj=proj, proj_bias=proj_bias, norm_gain=norm_gain, expert_ids=expert_ids, gate_codes=gate_codes, w_gate=w_gate, w_up=w_up, w_down_t=w_down_t, out_grad=out_grad)


epsilon = 1e-06

def silu_parts(pre_gate):
    sigmoid = jax.nn.sigmoid(pre_gate)
    return (pre_gate * sigmoid, sigmoid * (1.0 + pre_gate * (1.0 - sigmoid)))

def reference(feats, proj, proj_bias, norm_gain, expert_ids, gate_codes, w_gate, w_up, w_down_t, out_grad):
    hidden_in = (jnp.dot(feats, proj, preferred_element_type=jnp.float32) + proj_bias).astype(jnp.bfloat16)
    hidden_f = hidden_in.astype(jnp.float32)
    inv_rms = lax.rsqrt(lax.optimization_barrier(jnp.mean(hidden_f * hidden_f, axis=1, keepdims=True)) + epsilon)
    normed = (hidden_f * inv_rms * norm_gain).astype(jnp.bfloat16)
    devices_all = N_DP * N_EXPERT
    per_device = TOK_DEV * TOP
    device_ids = expert_ids.reshape(devices_all, per_device)
    onehot = (device_ids[:, :, None] == jnp.arange(EXPERTS, dtype=jnp.int32)).astype(jnp.int32)
    before = jnp.cumsum(onehot, axis=1) - onehot
    slot_index = lax.optimization_barrier(jnp.sum(before * onehot, axis=2)).astype(jnp.int32)
    device_index = jnp.arange(devices_all, dtype=jnp.int32)[:, None]
    slot_row = ((device_ids * devices_all + device_index) * CAP + slot_index).reshape(-1).astype(jnp.int32)
    token_id = (jnp.arange(TOKENS * TOP, dtype=jnp.int32) // TOP).astype(jnp.int32)
    slot_count = devices_all * CAP
    slot_token = jnp.zeros((EXPERTS * slot_count,), jnp.int32).at[slot_row].set(token_id).reshape(EXPERTS, slot_count)
    code_values = gate_codes.reshape(-1).astype(jnp.float32) / 64.0
    slot_weight = jnp.zeros((EXPERTS * slot_count,), jnp.float32).at[slot_row].set(code_values).reshape(EXPERTS, slot_count)

    def one_expert(running, packed):
        out_sum, grad_sum = running
        token_index, weights_here, gate_mat, up_mat, down_mat = packed
        slot_in = normed[token_index]
        slot_grad = out_grad[token_index]
        pre_gate = jnp.dot(slot_in, gate_mat, preferred_element_type=jnp.float32)
        pre_up = jnp.dot(slot_in, up_mat, preferred_element_type=jnp.float32)
        swished, slopes = silu_parts(pre_gate)
        mixed = (swished * pre_up).astype(jnp.bfloat16)
        expert_out = jnp.dot(mixed, down_mat.T, preferred_element_type=jnp.float32).astype(jnp.bfloat16)
        grad_hidden = jnp.dot(slot_grad, down_mat, preferred_element_type=jnp.float32)
        grad_gate = (grad_hidden * pre_up * slopes).astype(jnp.bfloat16)
        grad_up = (grad_hidden * swished).astype(jnp.bfloat16)
        expert_grad = (jnp.dot(grad_gate, gate_mat.T, preferred_element_type=jnp.float32) + jnp.dot(grad_up, up_mat.T, preferred_element_type=jnp.float32)).astype(jnp.bfloat16)
        out_sum = out_sum.at[token_index].add(weights_here[:, None] * expert_out.astype(jnp.float32))
        grad_sum = grad_sum.at[token_index].add(weights_here[:, None] * expert_grad.astype(jnp.float32))
        return ((out_sum, grad_sum), None)
    zero_rows = jnp.zeros((TOKENS, D), jnp.float32)
    (out_sum, grad_sum), unused = lax.scan(one_expert, (zero_rows, zero_rows), (slot_token, slot_weight, w_gate, w_up, w_down_t))
    layer_out = (hidden_f + out_sum).astype(jnp.bfloat16)
    scaled = grad_sum * norm_gain
    centre = lax.optimization_barrier(jnp.mean(hidden_f * scaled, axis=1, keepdims=True))
    input_grad = (out_grad.astype(jnp.float32) + inv_rms * scaled - hidden_f * inv_rms ** 3 * centre).astype(jnp.bfloat16)
    feat_grad = jnp.dot(input_grad, proj.T, preferred_element_type=jnp.float32).astype(jnp.bfloat16)
    return (layer_out, feat_grad)
```

```python
import jax
import jax.numpy as jnp
from jax import lax
from jax.experimental import pallas as pl
from jax.experimental.pallas import tpu as pltpu
from jax.sharding import PartitionSpec as P

CAP = 25
HALF = 56
SEND = 2 * HALF
WIN = 32
BACK = 104
SHIFT = 2
EPS = 1e-06
NO_SLOT = 200.0
BF = jnp.bfloat16
F32 = jnp.float32


def mm(a, b):
    return lax.dot_general(a, b, (((1,), (0,)), ((), ())), preferred_element_type=F32)


def mm_t(a, b):
    return lax.dot_general(a, b, (((1,), (1,)), ((), ())), preferred_element_type=F32)


def slot_rows(rows, offset, n_exp, slot):
    r = lax.broadcasted_iota(jnp.int32, (rows, 1), 0)
    chunk = (r * 1171) >> 16
    m = r - chunk * HALF - offset
    second = (m >= CAP).astype(jnp.int32)
    inside = (m >= 0) & (m < 2 * CAP)
    slot_of = jnp.where(inside, m - CAP * second, 99).astype(F32)
    lane = lax.broadcasted_iota(jnp.int32, (rows, n_exp), 1)
    pick = jnp.where(lane == 2 * chunk + second, 1.0, 0.0).astype(BF)
    return pick, mm(pick, slot) == slot_of


def prepare_kernel(
    feats, proj, bias, gain, ids, codes, grads, send, hidden, inv, mix_out, mix_grad
):
    sources = send.shape[0]
    rows = sources * HALF
    toks, width = grads.shape
    n_exp = 2 * sources
    lane = lax.broadcasted_iota(jnp.int32, (n_exp, toks), 0)
    member = jnp.zeros((n_exp, toks), F32)
    weight = jnp.zeros((n_exp, toks), F32)
    for k in range(ids.shape[0]):
        hit = lane == ids[k : k + 1, :]
        member = member + jnp.where(hit, 1.0, 0.0)
        weight = weight + jnp.where(hit, codes[k : k + 1, :].astype(F32) / 64.0, 0.0)
    weight = weight.astype(BF)
    earlier = lax.broadcasted_iota(jnp.int32, (toks, toks), 0) < lax.broadcasted_iota(
        jnp.int32, (toks, toks), 1
    )
    before = mm(member.astype(BF), jnp.where(earlier, 1.0, 0.0).astype(BF))
    slot = jnp.where(member > 0.5, before, NO_SLOT).astype(BF)
    pick, chosen = slot_rows(rows, 0, n_exp, slot)
    select = jnp.where(chosen, 1.0, 0.0).astype(BF)
    send[:, HALF:SEND, :] = mm(select, grads[...]).astype(BF).reshape(sources, HALF, width)
    h = (mm(feats[...], proj[...]) + bias[...]).astype(BF)
    hidden[...] = h
    hf = h.astype(F32)
    scale = lax.rsqrt(jnp.mean(hf * hf, axis=1, keepdims=True) + EPS)
    inv[...] = scale
    normed = (hf * scale * gain[...]).astype(BF)
    send[:, 0:HALF, :] = mm(select, normed).astype(BF).reshape(sources, HALF, width)
    mix_out[...] = jnp.where(chosen, mm(pick, weight), 0.0).T.astype(BF)
    pick, chosen = slot_rows(rows, SHIFT, n_exp, slot)
    mix_grad[...] = jnp.where(chosen, mm(pick, weight), 0.0).T.astype(BF)


def window(ref, start):
    part = ref[:, start : start + WIN, :]
    return part.reshape(part.shape[0] * WIN, part.shape[2])


def place(ref, outs, grads):
    n = ref.shape[0]
    width = ref.shape[2]
    first, second = (x.reshape(n, WIN, width) for x in outs)
    third, fourth = (pltpu.roll(x, SHIFT, 0).reshape(n, WIN, width) for x in grads)
    row = lax.broadcasted_iota(jnp.int32, (1, 8, 1), 1)

    def seam(count, a, b):
        return jnp.where(row < count, a[:, 24:32, :], b[:, 0:8, :]).astype(BF)

    ref[:, 0:24, :] = first[:, 0:24, :].astype(BF)
    ref[:, 24:32, :] = seam(1, first, second)
    ref[:, 32:48, :] = second[:, 8:24, :].astype(BF)
    ref[:, 48:56, :] = seam(2, second, third)
    ref[:, 56:72, :] = third[:, 8:24, :].astype(BF)
    ref[:, 72:80, :] = seam(3, third, fourth)
    ref[:, 80:104, :] = fourth[:, 8:32, :].astype(BF)


def matrix(buf, j):
    return buf[j].reshape(buf.shape[1] * buf.shape[2], buf.shape[3])


def expert_kernel(rows, weights, back, buf, sems):
    copies = {
        j: pltpu.make_async_copy(weights.at[:, j], buf.at[j], sems.at[j])
        for j in (0, 2, 4, 1, 3, 5)
    }
    for c in copies.values():
        c.start()
    outs, grads = [], []
    for e in range(2):
        x = window(rows, 24 * e)
        copies[e].wait()
        h = mm(x, matrix(buf, e))
        copies[2 + e].wait()
        u = mm(x, matrix(buf, 2 + e))
        sig = jax.nn.sigmoid(h)
        swished = h * sig
        upslope = u * (sig * (1.0 + h * (1.0 - sig)))
        copies[4 + e].wait()
        outs.append(mm_t((swished * u).astype(BF), matrix(buf, 4 + e)))
        g = mm(window(rows, HALF + 24 * e), matrix(buf, 4 + e))
        gate = (g * upslope).astype(BF)
        up = (g * swished).astype(BF)
        grads.append(mm_t(gate, matrix(buf, e)) + mm_t(up, matrix(buf, 2 + e)))
    place(back, outs, grads)


def combine_kernel(back, mix_out, mix_grad, hidden, inv, gain, grads, proj, out, feat_grad):
    n, _, width = back.shape
    hf = hidden[...].astype(F32)
    got = back[:, 0:HALF, :].reshape(n * HALF, width)
    out[...] = (hf + mm(mix_out[...], got)).astype(BF)
    got = back[:, BACK - HALF : BACK, :].reshape(n * HALF, width)
    scaled = mm(mix_grad[...], got) * gain[...]
    scale = inv[...]
    centre = jnp.mean(hf * scaled, axis=1, keepdims=True)
    total = grads[...].astype(F32) + scale * scaled - hf * (scale * scale * scale) * centre
    feat_grad[...] = mm_t(total.astype(BF), proj[...]).astype(BF)


def shape(dims, dtype):
    return jax.ShapeDtypeStruct(dims, dtype)


PARAMS = pltpu.CompilerParams(vmem_limit_bytes=56 * 1024 * 1024)
VMEM = pl.BlockSpec(memory_space=pltpu.VMEM)
ANY = pl.BlockSpec(memory_space=pl.ANY)


def shards(
    feats, proj, proj_bias, norm_gain, expert_ids, gate_codes, w_gate, w_up, w_down_t, out_grad
):
    toks, width = out_grad.shape
    sources = lax.axis_size("expert")
    local, part, ff = w_gate.shape
    bias, gain = proj_bias.reshape(1, width), norm_gain.reshape(1, width)
    stacked = jnp.concatenate([w_gate, w_up, w_down_t], axis=0)
    weights = lax.all_gather(stacked, "dp", axis=0, tiled=False)

    send, hidden, inv, mix_out, mix_grad = pl.pallas_call(
        prepare_kernel,
        out_shape=(
            shape((sources, SEND, width), BF),
            shape((toks, width), BF),
            shape((toks, 1), F32),
            shape((toks, sources * HALF), BF),
            shape((toks, sources * HALF), BF),
        ),
        in_specs=[VMEM] * 7,
        out_specs=(VMEM,) * 5,
        compiler_params=PARAMS,
        name="prepare",
    )(feats, proj, bias, gain, expert_ids.T, gate_codes.T, out_grad)
    received = lax.all_to_all(send, "expert", split_axis=0, concat_axis=0, tiled=True)
    results = pl.pallas_call(
        expert_kernel,
        out_shape=shape((sources, BACK, width), BF),
        in_specs=[VMEM, ANY],
        out_specs=VMEM,
        scratch_shapes=[
            pltpu.VMEM((3 * local, weights.shape[0], part, ff), BF),
            pltpu.SemaphoreType.DMA((3 * local,)),
        ],
        compiler_params=PARAMS,
        name="experts",
    )(received, weights)
    back = lax.all_to_all(results, "expert", split_axis=0, concat_axis=0, tiled=True)
    return pl.pallas_call(
        combine_kernel,
        out_shape=(shape((toks, width), BF), shape(feats.shape, BF)),
        in_specs=[VMEM] * 8,
        out_specs=(VMEM,) * 2,
        compiler_params=PARAMS,
        name="combine",
    )(back, mix_out, mix_grad, hidden, inv, gain, out_grad, proj)


def solution(mesh):
    tokens = P(("dp", "expert"), None)
    experts = P("expert", "dp", None)
    in_specs = (tokens, P(), P(), P(), tokens, tokens, experts, experts, experts, tokens)
    return jax.shard_map(
        shards, mesh=mesh, in_specs=in_specs, out_specs=(tokens, tokens), check_vma=False
    )
```

```python
import jax
import jax.numpy as jnp
from jax import lax
from jax.experimental import pallas as pl
from jax.experimental.pallas import tpu as pltpu
from jax.sharding import PartitionSpec as P

CHUNK = 104
KINDS = 4
MAIN = 24
LAST = KINDS * MAIN
EPS = 1e-06
NO_SLOT = 200.0
BF = jnp.bfloat16
F32 = jnp.float32


def mm(a, b):
    return lax.dot_general(a, b, (((1,), (0,)), ((), ())), preferred_element_type=F32)


def mm_t(a, b):
    return lax.dot_general(a, b, (((1,), (1,)), ((), ())), preferred_element_type=F32)


def prepare_kernel(feats, proj, bias, gain, ids, codes, grads, send, hidden, inv, mix):
    sources, _, width = send.shape
    rows = sources * CHUNK
    toks = grads.shape[0]
    n_exp = 2 * sources
    lane = lax.broadcasted_iota(jnp.int32, (n_exp, toks), 0)
    member = jnp.zeros((n_exp, toks), F32)
    weight = jnp.zeros((n_exp, toks), F32)
    for k in range(ids.shape[0]):
        hit = lane == ids[k : k + 1, :]
        member = member + jnp.where(hit, 1.0, 0.0)
        weight = weight + jnp.where(hit, codes[k : k + 1, :].astype(F32) / 64.0, 0.0)
    earlier = lax.broadcasted_iota(jnp.int32, (toks, toks), 0) < lax.broadcasted_iota(
        jnp.int32, (toks, toks), 1
    )
    before = mm(member.astype(BF), jnp.where(earlier, 1.0, 0.0).astype(BF))
    slot = jnp.where(member > 0.5, before, NO_SLOT).astype(BF)
    r = lax.broadcasted_iota(jnp.int32, (rows, 1), 0)
    chunk = (r * 40330) >> 22
    m = r - chunk * CHUNK
    kind = jnp.where(m < LAST, (m * 2731) >> 16, m - LAST)
    slot_of = jnp.where(m < LAST, m - MAIN * kind, jnp.where(m < LAST + KINDS, MAIN, 99))
    pick = jnp.where(
        lax.broadcasted_iota(jnp.int32, (rows, n_exp), 1) == 2 * chunk + (kind & 1), 1.0, 0.0
    ).astype(BF)
    chosen = jnp.where(mm(pick, slot) == slot_of.astype(F32), 1.0, 0.0)
    of_token = jnp.where(kind < 2, chosen, 0.0)
    of_grad = jnp.where(kind < 2, 0.0, chosen)
    spread = mm(pick, weight.astype(BF))
    mix[0:toks, :] = (spread * of_token).T.astype(BF)
    mix[toks : 2 * toks, :] = (spread * of_grad).T.astype(BF)
    from_grads = mm(of_grad.astype(BF), grads[...])
    h = (mm(feats[...], proj[...]) + bias[...]).astype(BF)
    hidden[...] = h
    hf = h.astype(F32)
    scale = lax.rsqrt(jnp.mean(hf * hf, axis=1, keepdims=True) + EPS)
    inv[...] = scale
    normed = (hf * scale * gain[...]).astype(BF)
    sent = from_grads + mm(of_token.astype(BF), normed)
    send[...] = sent.reshape(sources, CHUNK, width).astype(BF)


def arrange_kernel(received, rows):
    sources, _, width = received.shape
    last = received[:, LAST:CHUNK, :].astype(F32)
    for k in range(KINDS):
        part = received[:, MAIN * k : MAIN * (k + 1), :].astype(F32)
        rows[k, 0 : sources * MAIN, :] = part.reshape(sources * MAIN, width).astype(BF)
        rows[k, sources * MAIN :, :] = last[:, k, :].astype(BF)


def expert_kernel(rows, weights, back, buf, mixed, d_gate, d_up, sems):
    sources, _, width = back.shape
    total = rows.shape[1]
    shards_of, part, ff = buf.shape[1:]
    half = total // 32 * 16
    blocks = (slice(0, half), slice(half, total))
    copies = {
        j: pltpu.make_async_copy(weights.at[:, j], buf.at[j], sems.at[j])
        for j in (0, 2, 4, 1, 3, 5)
    }
    for c in copies.values():
        c.start()
    ready, last = set(), {}

    def matrix(j):
        if j not in ready:
            copies[j].wait()
            ready.add(j)
        return buf[j].reshape(shards_of * part, ff)

    def store(kind, result):
        main = result[0 : sources * MAIN].reshape(sources, MAIN, width)
        back[:, MAIN * kind : MAIN * (kind + 1), :] = main.astype(BF)
        last[kind] = result[sources * MAIN :].reshape(sources, 1, width)

    def first_products(e):
        h = [mm(rows[e, at, :], matrix(e)) for at in blocks]
        u = [mm(rows[e, at, :], matrix(2 + e)) for at in blocks]
        g = [mm(rows[2 + e, at, :], matrix(4 + e)) for at in blocks]
        return h, u, g

    def elementwise(e, i, h, u, g):
        sig = jax.nn.sigmoid(h[i])
        swished = h[i] * sig
        mixed[e, blocks[i], :] = (swished * u[i]).astype(BF)
        d_gate[e, blocks[i], :] = (g[i] * (u[i] * (sig * (1.0 + h[i] * (1.0 - sig))))).astype(BF)
        d_up[e, blocks[i], :] = (g[i] * swished).astype(BF)

    def second_products(e):
        store(e, mm_t(mixed[e], matrix(4 + e)))
        store(2 + e, mm_t(d_gate[e], matrix(e)) + mm_t(d_up[e], matrix(2 + e)))

    for e in range(2):
        products = first_products(e)
        for i in range(2):
            elementwise(e, i, *products)
        second_products(e)
    row = lax.broadcasted_iota(jnp.int32, (1, CHUNK - LAST, 1), 1)
    rest = jnp.zeros((sources, CHUNK - LAST, width), F32)
    for kind in range(KINDS):
        rest = jnp.where(row == kind, last[kind], rest)
    back[:, LAST:CHUNK, :] = rest.astype(BF)


def stack_kernel(w_gate, w_up, w_down_t, out, sems):
    local = w_gate.shape[0]
    copies = [
        pltpu.make_async_copy(w, out.at[i * local : (i + 1) * local], sems.at[i])
        for i, w in enumerate((w_gate, w_up, w_down_t))
    ]
    for c in copies:
        c.start()
    for c in copies:
        c.wait()


def combine_kernel(back, mix, hidden, inv, gain, grads, proj, out, feat_grad):
    n, _, width = back.shape
    toks = hidden.shape[0]
    hf = hidden[...].astype(F32)
    sums = mm(mix[...], back[...].reshape(n * CHUNK, width))
    out[...] = (hf + sums[0:toks]).astype(BF)
    scaled = sums[toks : 2 * toks] * gain[...]
    scale = inv[...]
    centre = jnp.mean(hf * scaled, axis=1, keepdims=True)
    total = grads[...].astype(F32) + scale * scaled - hf * (scale * scale * scale) * centre
    feat_grad[...] = mm_t(total.astype(BF), proj[...]).astype(BF)


def shape(dims, dtype):
    return jax.ShapeDtypeStruct(dims, dtype)


def params(mib):
    return pltpu.CompilerParams(vmem_limit_bytes=mib * 1024 * 1024)


VMEM = pl.BlockSpec(memory_space=pltpu.VMEM)
HBM = pl.BlockSpec(memory_space=pltpu.HBM)


def shards(
    feats, proj, proj_bias, norm_gain, expert_ids, gate_codes, w_gate, w_up, w_down_t, out_grad
):
    toks, width = out_grad.shape
    sources = lax.axis_size("expert")
    local, part, ff = w_gate.shape
    bias, gain = proj_bias.reshape(1, width), norm_gain.reshape(1, width)
    stacked = pl.pallas_call(
        stack_kernel,
        out_shape=shape((3 * local, part, ff), BF),
        in_specs=[HBM] * 3,
        out_specs=HBM,
        scratch_shapes=[pltpu.SemaphoreType.DMA((3,))],
        compiler_params=params(16),
        name="stack",
    )(w_gate, w_up, w_down_t)
    weights = lax.all_gather(stacked, "dp", axis=0, tiled=False)

    send, hidden, inv, mix = pl.pallas_call(
        prepare_kernel,
        out_shape=(
            shape((sources, CHUNK, width), BF),
            shape((toks, width), BF),
            shape((toks, 1), F32),
            shape((2 * toks, sources * CHUNK), BF),
        ),
        in_specs=[VMEM] * 7,
        out_specs=(VMEM,) * 4,
        compiler_params=params(28),
        name="prepare",
    )(feats, proj, bias, gain, expert_ids.T, gate_codes.T, out_grad)
    received = lax.all_to_all(send, "expert", split_axis=0, concat_axis=0, tiled=True)
    slots = sources * (MAIN + 1)
    rows = pl.pallas_call(
        arrange_kernel,
        out_shape=shape((KINDS, slots, width), BF),
        in_specs=[VMEM],
        out_specs=VMEM,
        compiler_params=params(28),
        name="arrange",
    )(received)
    results = pl.pallas_call(
        expert_kernel,
        out_shape=shape((sources, CHUNK, width), BF),
        in_specs=[VMEM, HBM],
        out_specs=VMEM,
        scratch_shapes=[
            pltpu.VMEM((3 * local, weights.shape[0], part, ff), BF),
            pltpu.VMEM((local, slots, ff), BF),
            pltpu.VMEM((local, slots, ff), BF),
            pltpu.VMEM((local, slots, ff), BF),
            pltpu.SemaphoreType.DMA((3 * local,)),
        ],
        compiler_params=params(46),
        name="experts",
    )(rows, weights)
    back = lax.all_to_all(results, "expert", split_axis=0, concat_axis=0, tiled=True)
    return pl.pallas_call(
        combine_kernel,
        out_shape=(shape((toks, width), BF), shape(feats.shape, BF)),
        in_specs=[VMEM] * 7,
        out_specs=(VMEM,) * 2,
        compiler_params=params(28),
        name="combine",
    )(back, mix, hidden, inv, gain, out_grad, proj)


def solution(mesh):
    tokens = P(("dp", "expert"), None)
    experts = P("expert", "dp", None)
    in_specs = (tokens, P(), P(), P(), tokens, tokens, experts, experts, experts, tokens)
    return jax.shard_map(
        shards, mesh=mesh, in_specs=in_specs, out_specs=(tokens, tokens), check_vma=False
    )
```

```python
import jax
import jax.numpy as jnp
from jax import lax
from jax.experimental import pallas as pl
from jax.experimental.pallas import tpu as pltpu
from jax.sharding import PartitionSpec as P

CHUNK = 104
KINDS = 4
MAIN = 24
LAST = KINDS * MAIN
EPS = 1e-06
NO_SLOT = 200.0
BF = jnp.bfloat16
F32 = jnp.float32


def mm(a, b):
    return lax.dot_general(a, b, (((1,), (0,)), ((), ())), preferred_element_type=F32)


def mm_t(a, b):
    return lax.dot_general(a, b, (((1,), (1,)), ((), ())), preferred_element_type=F32)


def prepare_kernel(
    feats, proj, bias, gain, ids, codes, grads, send, hidden, inv, mix, mix_last
):
    sources, _, width = send.shape
    rows = sources * CHUNK
    toks = grads.shape[0]
    n_exp = 2 * sources
    lane = lax.broadcasted_iota(jnp.int32, (n_exp, toks), 0)
    member = jnp.zeros((n_exp, toks), F32)
    weight = jnp.zeros((n_exp, toks), F32)
    for k in range(ids.shape[0]):
        hit = lane == ids[k : k + 1, :]
        member = member + jnp.where(hit, 1.0, 0.0)
        weight = weight + jnp.where(hit, codes[k : k + 1, :].astype(F32) / 64.0, 0.0)
    earlier = lax.broadcasted_iota(jnp.int32, (toks, toks), 0) < lax.broadcasted_iota(
        jnp.int32, (toks, toks), 1
    )
    before = mm(member.astype(BF), jnp.where(earlier, 1.0, 0.0).astype(BF))
    slot = jnp.where(member > 0.5, before, NO_SLOT).astype(BF)
    r = lax.broadcasted_iota(jnp.int32, (rows, 1), 0)
    chunk = (r * 40330) >> 22
    m = r - chunk * CHUNK
    kind = jnp.where(m < LAST, (m * 2731) >> 16, m - LAST)
    slot_of = jnp.where(m < LAST, m - MAIN * kind, jnp.where(m < LAST + KINDS, MAIN, 99))
    pick = jnp.where(
        lax.broadcasted_iota(jnp.int32, (rows, n_exp), 1) == 2 * chunk + (kind & 1), 1.0, 0.0
    ).astype(BF)
    chosen = jnp.where(mm(pick, slot) == slot_of.astype(F32), 1.0, 0.0)
    of_token = jnp.where(kind < 2, chosen, 0.0)
    of_grad = jnp.where(kind < 2, 0.0, chosen)
    spread = mm(pick, weight.astype(BF))
    spread = (spread * chosen).reshape(sources, CHUNK, toks)
    side = LAST // 2
    for i in range(2):
        part = spread[:, side * i : side * (i + 1), :]
        mix[i] = part.reshape(sources * side, toks).T.astype(BF)
    part = spread[:, LAST:CHUNK, :]
    row = lax.broadcasted_iota(jnp.int32, (1, CHUNK - LAST, 1), 1)
    for i in range(2):
        mine = jnp.where((row < 2) == (i == 0), part, 0.0)
        mix_last[i] = mine.reshape(sources * (CHUNK - LAST), toks).T.astype(BF)
    from_grads = mm(of_grad.astype(BF), grads[...])
    h = (mm(feats[...], proj[...]) + bias[...]).astype(BF)
    hidden[...] = h
    hf = h.astype(F32)
    scale = lax.rsqrt(jnp.mean(hf * hf, axis=1, keepdims=True) + EPS)
    inv[...] = scale
    normed = (hf * scale * gain[...]).astype(BF)
    sent = from_grads + mm(of_token.astype(BF), normed)
    send[...] = sent.reshape(sources, CHUNK, width).astype(BF)


def arrange_kernel(received, rows):
    sources, _, width = received.shape
    last = received[:, LAST:CHUNK, :].astype(F32)
    for k in range(KINDS):
        part = received[:, MAIN * k : MAIN * (k + 1), :].astype(F32)
        rows[k, 0 : sources * MAIN, :] = part.reshape(sources * MAIN, width).astype(BF)
        rows[k, sources * MAIN :, :] = last[:, k, :].astype(BF)


def expert_kernel(rows, weights, back, buf, mixed, d_gate, d_up, sems):
    sources, _, width = back.shape
    total = rows.shape[1]
    shards_of, part, ff = buf.shape[1:]
    half = total // 32 * 16
    blocks = (slice(0, half), slice(half, total))
    copies = {
        j: pltpu.make_async_copy(weights.at[:, j], buf.at[j], sems.at[j])
        for j in (0, 2, 4, 1, 3, 5)
    }
    for c in copies.values():
        c.start()
    ready, last = set(), {}

    def matrix(j):
        if j not in ready:
            copies[j].wait()
            ready.add(j)
        return buf[j].reshape(shards_of * part, ff)

    def store(kind, result):
        main = result[0 : sources * MAIN].reshape(sources, MAIN, width)
        back[:, MAIN * kind : MAIN * (kind + 1), :] = main.astype(BF)
        last[kind] = result[sources * MAIN :].reshape(sources, 1, width)

    def first_products(e):
        h = [mm(rows[e, at, :], matrix(e)) for at in blocks]
        u = [mm(rows[e, at, :], matrix(2 + e)) for at in blocks]
        g = [mm(rows[2 + e, at, :], matrix(4 + e)) for at in blocks]
        return h, u, g

    def elementwise(e, i, h, u, g):
        sig = jax.nn.sigmoid(h[i])
        swished = h[i] * sig
        mixed[e, blocks[i], :] = (swished * u[i]).astype(BF)
        d_gate[e, blocks[i], :] = (g[i] * (u[i] * (sig * (1.0 + h[i] * (1.0 - sig))))).astype(BF)
        d_up[e, blocks[i], :] = (g[i] * swished).astype(BF)

    def second_products(e):
        store(e, mm_t(mixed[e], matrix(4 + e)))
        store(2 + e, mm_t(d_gate[e], matrix(e)) + mm_t(d_up[e], matrix(2 + e)))

    for e in range(2):
        products = first_products(e)
        for i in range(2):
            elementwise(e, i, *products)
        second_products(e)
    row = lax.broadcasted_iota(jnp.int32, (1, CHUNK - LAST, 1), 1)
    rest = jnp.zeros((sources, CHUNK - LAST, width), F32)
    for kind in range(KINDS):
        rest = jnp.where(row == kind, last[kind], rest)
    back[:, LAST:CHUNK, :] = rest.astype(BF)


def stack_kernel(w_gate, w_up, w_down_t, out, sems):
    local = w_gate.shape[0]
    copies = [
        pltpu.make_async_copy(w, out.at[i * local : (i + 1) * local], sems.at[i])
        for i, w in enumerate((w_gate, w_up, w_down_t))
    ]
    for c in copies:
        c.start()
    for c in copies:
        c.wait()


def combine_kernel(
    back, mix, mix_last, hidden, inv, gain, grads, proj, out, feat_grad
):
    n, _, width = back.shape
    side = LAST // 2
    last = back[:, LAST:CHUNK, :].reshape(n * (CHUNK - LAST), width)

    def total_of(i):
        main = back[:, side * i : side * (i + 1), :].reshape(n * side, width)
        return mm(mix[i], main) + mm(mix_last[i], last)

    hf = hidden[...].astype(F32)
    out[...] = (hf + total_of(0)).astype(BF)
    scaled = total_of(1) * gain[...]
    scale = inv[...]
    centre = jnp.mean(hf * scaled, axis=1, keepdims=True)
    total = grads[...].astype(F32) + scale * scaled - hf * (scale * scale * scale) * centre
    feat_grad[...] = mm_t(total.astype(BF), proj[...]).astype(BF)


def shape(dims, dtype):
    return jax.ShapeDtypeStruct(dims, dtype)


def params(mib):
    return pltpu.CompilerParams(vmem_limit_bytes=mib * 1024 * 1024)


VMEM = pl.BlockSpec(memory_space=pltpu.VMEM)
HBM = pl.BlockSpec(memory_space=pltpu.HBM)


def shards(
    feats, proj, proj_bias, norm_gain, expert_ids, gate_codes, w_gate, w_up, w_down_t, out_grad
):
    toks, width = out_grad.shape
    sources = lax.axis_size("expert")
    local, part, ff = w_gate.shape
    bias, gain = proj_bias.reshape(1, width), norm_gain.reshape(1, width)
    stacked = pl.pallas_call(
        stack_kernel,
        out_shape=shape((3 * local, part, ff), BF),
        in_specs=[HBM] * 3,
        out_specs=HBM,
        scratch_shapes=[pltpu.SemaphoreType.DMA((3,))],
        compiler_params=params(60),
        name="stack",
    )(w_gate, w_up, w_down_t)
    weights = lax.all_gather(stacked, "dp", axis=0, tiled=False)

    send, hidden, inv, mix, mix_last = pl.pallas_call(
        prepare_kernel,
        out_shape=(
            shape((sources, CHUNK, width), BF),
            shape((toks, width), BF),
            shape((toks, 1), F32),
            shape((2, toks, sources * LAST // 2), BF),
            shape((2, toks, sources * (CHUNK - LAST)), BF),
        ),
        in_specs=[VMEM] * 7,
        out_specs=(VMEM,) * 5,
        compiler_params=params(28),
        name="prepare",
    )(feats, proj, bias, gain, expert_ids.T, gate_codes.T, out_grad)
    received = lax.all_to_all(send, "expert", split_axis=0, concat_axis=0, tiled=True)
    slots = sources * (MAIN + 1)
    rows = pl.pallas_call(
        arrange_kernel,
        out_shape=shape((KINDS, slots, width), BF),
        in_specs=[VMEM],
        out_specs=VMEM,
        compiler_params=params(28),
        name="arrange",
    )(received)
    results = pl.pallas_call(
        expert_kernel,
        out_shape=shape((sources, CHUNK, width), BF),
        in_specs=[VMEM, HBM],
        out_specs=VMEM,
        scratch_shapes=[
            pltpu.VMEM((3 * local, weights.shape[0], part, ff), BF),
            pltpu.VMEM((local, slots, ff), BF),
            pltpu.VMEM((local, slots, ff), BF),
            pltpu.VMEM((local, slots, ff), BF),
            pltpu.SemaphoreType.DMA((3 * local,)),
        ],
        compiler_params=params(46),
        name="experts",
    )(rows, weights)
    back = lax.all_to_all(results, "expert", split_axis=0, concat_axis=0, tiled=True)
    return pl.pallas_call(
        combine_kernel,
        out_shape=(shape((toks, width), BF), shape(feats.shape, BF)),
        in_specs=[VMEM] * 8,
        out_specs=(VMEM,) * 2,
        compiler_params=params(28),
        name="combine",
    )(back, mix, mix_last, hidden, inv, gain, out_grad, proj)


def solution(mesh):
    tokens = P(("dp", "expert"), None)
    experts = P("expert", "dp", None)
    in_specs = (tokens, P(), P(), P(), tokens, tokens, experts, experts, experts, tokens)
    return jax.shard_map(
        shards, mesh=mesh, in_specs=in_specs, out_specs=(tokens, tokens), check_vma=False
    )
```

```python
import jax
import jax.numpy as jnp
from jax import lax
from jax.experimental import pallas as pl
from jax.experimental.pallas import tpu as pltpu
from jax.sharding import PartitionSpec as P

CHUNK = 104
KINDS = 4
MAIN = 24
LAST = KINDS * MAIN
EPS = 1e-06
NO_SLOT = 200.0
BF = jnp.bfloat16
F32 = jnp.float32


def mm(a, b):
    return lax.dot_general(a, b, (((1,), (0,)), ((), ())), preferred_element_type=F32)


def mm_t(a, b):
    return lax.dot_general(a, b, (((1,), (1,)), ((), ())), preferred_element_type=F32)


def prepare_kernel(
    feats, proj, bias, gain, ids, codes, grads, send, hidden, inv, mix, mix_last
):
    sources, _, width = send.shape
    rows = sources * CHUNK
    toks = grads.shape[0]
    n_exp = 2 * sources
    lane = lax.broadcasted_iota(jnp.int32, (n_exp, toks), 0)
    member = jnp.zeros((n_exp, toks), F32)
    weight = jnp.zeros((n_exp, toks), F32)
    for k in range(ids.shape[0]):
        hit = lane == ids[k : k + 1, :]
        member = member + jnp.where(hit, 1.0, 0.0)
        weight = weight + jnp.where(hit, codes[k : k + 1, :].astype(F32) / 64.0, 0.0)
    earlier = lax.broadcasted_iota(jnp.int32, (toks, toks), 0) < lax.broadcasted_iota(
        jnp.int32, (toks, toks), 1
    )
    before = mm(member.astype(BF), jnp.where(earlier, 1.0, 0.0).astype(BF))
    slot = jnp.where(member > 0.5, before, NO_SLOT).astype(BF)
    r = lax.broadcasted_iota(jnp.int32, (rows, 1), 0)
    chunk = (r * 40330) >> 22
    m = r - chunk * CHUNK
    kind = jnp.where(m < LAST, (m * 2731) >> 16, m - LAST)
    slot_of = jnp.where(m < LAST, m - MAIN * kind, jnp.where(m < LAST + KINDS, MAIN, 99))
    pick = jnp.where(
        lax.broadcasted_iota(jnp.int32, (rows, n_exp), 1) == 2 * chunk + (kind & 1), 1.0, 0.0
    ).astype(BF)
    chosen = jnp.where(mm(pick, slot) == slot_of.astype(F32), 1.0, 0.0)
    of_token = jnp.where(kind < 2, chosen, 0.0)
    of_grad = jnp.where(kind < 2, 0.0, chosen)
    spread = mm(pick, weight.astype(BF))
    spread = (spread * chosen).reshape(sources, CHUNK, toks)
    side = LAST // 2
    for i in range(2):
        part = spread[:, side * i : side * (i + 1), :]
        mix[i] = part.reshape(sources * side, toks).T.astype(BF)
    part = spread[:, LAST:CHUNK, :]
    row = lax.broadcasted_iota(jnp.int32, (1, CHUNK - LAST, 1), 1)
    for i in range(2):
        mine = jnp.where((row < 2) == (i == 0), part, 0.0)
        mix_last[i] = mine.reshape(sources * (CHUNK - LAST), toks).T.astype(BF)
    from_grads = mm(of_grad.astype(BF), grads[...])
    h = (mm(feats[...], proj[...]) + bias[...]).astype(BF)
    hidden[...] = h
    hf = h.astype(F32)
    scale = lax.rsqrt(jnp.mean(hf * hf, axis=1, keepdims=True) + EPS)
    inv[...] = scale
    normed = (hf * scale * gain[...]).astype(BF)
    sent = from_grads + mm(of_token.astype(BF), normed)
    send[...] = sent.reshape(sources, CHUNK, width).astype(BF)


def arrange_kernel(received, rows):
    sources, _, width = received.shape
    last = received[:, LAST:CHUNK, :].astype(F32)
    for k in range(KINDS):
        part = received[:, MAIN * k : MAIN * (k + 1), :].astype(F32)
        rows[k, 0 : sources * MAIN, :] = part.reshape(sources * MAIN, width).astype(BF)
        rows[k, sources * MAIN :, :] = last[:, k, :].astype(BF)


def expert_kernel(rows, weights, back, buf, mixed, d_gate, d_up, sems):
    sources, _, width = back.shape
    total = rows.shape[1]
    shards_of, part, ff = buf.shape[1:]
    half = total // 32 * 16
    blocks = (slice(0, half), slice(half, total))
    copies = {
        j: pltpu.make_async_copy(weights.at[:, j], buf.at[j], sems.at[j])
        for j in (0, 2, 4, 1, 3, 5)
    }
    for c in copies.values():
        c.start()
    ready, last = set(), {}

    def matrix(j):
        if j not in ready:
            copies[j].wait()
            ready.add(j)
        return buf[j].reshape(shards_of * part, ff)

    def store(kind, result):
        main = result[0 : sources * MAIN].reshape(sources, MAIN, width)
        back[:, MAIN * kind : MAIN * (kind + 1), :] = main.astype(BF)
        last[kind] = result[sources * MAIN :].reshape(sources, 1, width)

    def first_products(e):
        h = [mm(rows[e, at, :], matrix(e)) for at in blocks]
        u = [mm(rows[e, at, :], matrix(2 + e)) for at in blocks]
        g = [mm(rows[2 + e, at, :], matrix(4 + e)) for at in blocks]
        return h, u, g

    def elementwise(e, i, h, u, g):
        sig = jax.nn.sigmoid(h[i])
        swished = h[i] * sig
        mixed[e, blocks[i], :] = (swished * u[i]).astype(BF)
        d_gate[e, blocks[i], :] = (g[i] * (u[i] * (sig * (1.0 + h[i] * (1.0 - sig))))).astype(BF)
        d_up[e, blocks[i], :] = (g[i] * swished).astype(BF)

    def second_products(e):
        store(e, mm_t(mixed[e], matrix(4 + e)))
        store(2 + e, mm_t(d_gate[e], matrix(e)) + mm_t(d_up[e], matrix(2 + e)))

    for e in range(2):
        products = first_products(e)
        for i in range(2):
            elementwise(e, i, *products)
        second_products(e)
    row = lax.broadcasted_iota(jnp.int32, (1, CHUNK - LAST, 1), 1)
    rest = jnp.zeros((sources, CHUNK - LAST, width), F32)
    for kind in range(KINDS):
        rest = jnp.where(row == kind, last[kind], rest)
    back[:, LAST:CHUNK, :] = rest.astype(BF)


def stack_kernel(w_gate, w_up, w_down_t, out, sems):
    local = w_gate.shape[0]
    copies = [
        pltpu.make_async_copy(w, out.at[i * local : (i + 1) * local], sems.at[i])
        for i, w in enumerate((w_gate, w_up, w_down_t))
    ]
    for c in copies:
        c.start()
    for c in copies:
        c.wait()


def combine_kernel(
    back, mix, mix_last, hidden, inv, gain, grads, proj, out, feat_grad
):
    n, _, width = back.shape
    side = LAST // 2
    last = back[:, LAST:CHUNK, :].reshape(n * (CHUNK - LAST), width)

    def total_of(i):
        main = back[:, side * i : side * (i + 1), :].reshape(n * side, width)
        return mm(mix[i], main) + mm(mix_last[i], last)

    hf = hidden[...].astype(F32)
    out[...] = (hf + total_of(0)).astype(BF)
    scaled = total_of(1) * gain[...]
    scale = inv[...]
    centre = jnp.mean(hf * scaled, axis=1, keepdims=True)
    total = grads[...].astype(F32) + scale * scaled - hf * (scale * scale * scale) * centre
    feat_grad[...] = mm_t(total.astype(BF), proj[...]).astype(BF)


def shape(dims, dtype):
    return jax.ShapeDtypeStruct(dims, dtype)


def params(mib):
    return pltpu.CompilerParams(vmem_limit_bytes=mib * 1024 * 1024)


VMEM = pl.BlockSpec(memory_space=pltpu.VMEM)
HBM = pl.BlockSpec(memory_space=pltpu.HBM)


def shards(
    feats, proj, proj_bias, norm_gain, expert_ids, gate_codes, w_gate, w_up, w_down_t, out_grad
):
    toks, width = out_grad.shape
    sources = lax.axis_size("expert")
    local, part, ff = w_gate.shape
    bias, gain = proj_bias.reshape(1, width), norm_gain.reshape(1, width)
    stacked = pl.pallas_call(
        stack_kernel,
        out_shape=shape((3 * local, part, ff), BF),
        in_specs=[HBM] * 3,
        out_specs=HBM,
        scratch_shapes=[pltpu.SemaphoreType.DMA((3,))],
        compiler_params=params(16),
        name="stack",
    )(w_gate, w_up, w_down_t)
    weights = lax.all_gather(stacked, "dp", axis=0, tiled=False)

    send, hidden, inv, mix, mix_last = pl.pallas_call(
        prepare_kernel,
        out_shape=(
            shape((sources, CHUNK, width), BF),
            shape((toks, width), BF),
            shape((toks, 1), F32),
            shape((2, toks, sources * LAST // 2), BF),
            shape((2, toks, sources * (CHUNK - LAST)), BF),
        ),
        in_specs=[VMEM] * 7,
        out_specs=(VMEM,) * 5,
        compiler_params=params(28),
        name="prepare",
    )(feats, proj, bias, gain, expert_ids.T, gate_codes.T, out_grad)
    received = lax.all_to_all(send, "expert", split_axis=0, concat_axis=0, tiled=True)
    slots = sources * (MAIN + 1)
    rows = pl.pallas_call(
        arrange_kernel,
        out_shape=shape((KINDS, slots, width), BF),
        in_specs=[VMEM],
        out_specs=VMEM,
        compiler_params=params(28),
        name="arrange",
    )(received)
    results = pl.pallas_call(
        expert_kernel,
        out_shape=shape((sources, CHUNK, width), BF),
        in_specs=[VMEM, HBM],
        out_specs=VMEM,
        scratch_shapes=[
            pltpu.VMEM((3 * local, weights.shape[0], part, ff), BF),
            pltpu.VMEM((local, slots, ff), BF),
            pltpu.VMEM((local, slots, ff), BF),
            pltpu.VMEM((local, slots, ff), BF),
            pltpu.SemaphoreType.DMA((3 * local,)),
        ],
        compiler_params=params(46),
        name="experts",
    )(rows, weights)
    back = lax.all_to_all(results, "expert", split_axis=0, concat_axis=0, tiled=True)
    return pl.pallas_call(
        combine_kernel,
        out_shape=(shape((toks, width), BF), shape(feats.shape, BF)),
        in_specs=[VMEM] * 8,
        out_specs=(VMEM,) * 2,
        compiler_params=params(28),
        name="combine",
    )(back, mix, mix_last, hidden, inv, gain, out_grad, proj)


def solution(mesh):
    tokens = P(("dp", "expert"), None)
    experts = P("expert", "dp", None)
    in_specs = (tokens, P(), P(), P(), tokens, tokens, experts, experts, experts, tokens)
    return jax.shard_map(
        shards, mesh=mesh, in_specs=in_specs, out_specs=(tokens, tokens), check_vma=False
    )
```

```python
import jax
import jax.numpy as jnp
from jax import lax
from jax.experimental import pallas as pl
from jax.experimental.pallas import tpu as pltpu
from jax.sharding import PartitionSpec as P

CHUNK = 104
KINDS = 4
MAIN = 24
LAST = KINDS * MAIN
EPS = 1e-06
NO_SLOT = 200.0
BF = jnp.bfloat16
F32 = jnp.float32


def mm(a, b):
    return lax.dot_general(a, b, (((1,), (0,)), ((), ())), preferred_element_type=F32)


def mm_t(a, b):
    return lax.dot_general(a, b, (((1,), (1,)), ((), ())), preferred_element_type=F32)


def prepare_kernel(
    feats, proj, bias, gain, ids, codes, grads, send, hidden, inv, mix, mix_last
):
    sources, _, width = send.shape
    rows = sources * CHUNK
    toks = grads.shape[0]
    n_exp = 2 * sources
    lane = lax.broadcasted_iota(jnp.int32, (n_exp, toks), 0)
    member = jnp.zeros((n_exp, toks), F32)
    weight = jnp.zeros((n_exp, toks), F32)
    for k in range(ids.shape[0]):
        hit = lane == ids[k : k + 1, :]
        member = member + jnp.where(hit, 1.0, 0.0)
        weight = weight + jnp.where(hit, codes[k : k + 1, :].astype(F32) / 64.0, 0.0)
    earlier = lax.broadcasted_iota(jnp.int32, (toks, toks), 0) < lax.broadcasted_iota(
        jnp.int32, (toks, toks), 1
    )
    before = mm(member.astype(BF), jnp.where(earlier, 1.0, 0.0).astype(BF))
    slot = jnp.where(member > 0.5, before, NO_SLOT).astype(BF)
    r = lax.broadcasted_iota(jnp.int32, (rows, 1), 0)
    chunk = (r * 40330) >> 22
    m = r - chunk * CHUNK
    kind = jnp.where(m < LAST, (m * 2731) >> 16, m - LAST)
    slot_of = jnp.where(m < LAST, m - MAIN * kind, jnp.where(m < LAST + KINDS, MAIN, 99))
    pick = jnp.where(
        lax.broadcasted_iota(jnp.int32, (rows, n_exp), 1) == 2 * chunk + (kind & 1), 1.0, 0.0
    ).astype(BF)
    chosen = jnp.where(mm(pick, slot) == slot_of.astype(F32), 1.0, 0.0)
    of_token = jnp.where(kind < 2, chosen, 0.0)
    of_grad = jnp.where(kind < 2, 0.0, chosen)
    spread = mm(pick, weight.astype(BF))
    spread = (spread * chosen).reshape(sources, CHUNK, toks)
    side = LAST // 2
    for i in range(2):
        part = spread[:, side * i : side * (i + 1), :]
        mix[i] = part.reshape(sources * side, toks).T.astype(BF)
    part = spread[:, LAST:CHUNK, :]
    row = lax.broadcasted_iota(jnp.int32, (1, CHUNK - LAST, 1), 1)
    for i in range(2):
        mine = jnp.where((row < 2) == (i == 0), part, 0.0)
        mix_last[i] = mine.reshape(sources * (CHUNK - LAST), toks).T.astype(BF)
    from_grads = mm(of_grad.astype(BF), grads[...])
    h = (mm(feats[...], proj[...]) + bias[...]).astype(BF)
    hidden[...] = h
    hf = h.astype(F32)
    scale = lax.rsqrt(jnp.mean(hf * hf, axis=1, keepdims=True) + EPS)
    inv[...] = scale
    normed = (hf * scale * gain[...]).astype(BF)
    sent = from_grads + mm(of_token.astype(BF), normed)
    send[...] = sent.reshape(sources, CHUNK, width).astype(BF)


def arrange_kernel(received, rows):
    sources, _, width = received.shape
    last = received[:, LAST:CHUNK, :].astype(F32)
    for k in range(KINDS):
        part = received[:, MAIN * k : MAIN * (k + 1), :].astype(F32)
        rows[k, 0 : sources * MAIN, :] = part.reshape(sources * MAIN, width).astype(BF)
        rows[k, sources * MAIN :, :] = last[:, k, :].astype(BF)


def expert_kernel(rows, weights, back, wide, down, mixed, d_wide, sems):
    sources, _, width = back.shape
    total = rows.shape[1]
    shards_of, part, ff = down.shape[1:]
    half = total // 32 * 16
    blocks = (slice(0, half), slice(half, total))
    copies = {}
    for e in range(2):
        for j, to in (
            (e, wide.at[e, :, :, 0:ff]),
            (2 + e, wide.at[e, :, :, ff : 2 * ff]),
            (4 + e, down.at[e]),
        ):
            copies[j] = pltpu.make_async_copy(weights.at[:, j], to, sems.at[j])
            copies[j].start()
    last = {}

    def gate_up(e, at):
        return wide[e, :, :, at].reshape(shards_of * part, at.stop - at.start)

    def store(kind, result):
        main = result[0 : sources * MAIN].reshape(sources, MAIN, width)
        back[:, MAIN * kind : MAIN * (kind + 1), :] = main.astype(BF)
        last[kind] = result[sources * MAIN :].reshape(sources, 1, width)

    for e in range(2):
        copies[e].wait()
        h = [mm(rows[e, at, :], gate_up(e, slice(0, ff))) for at in blocks]
        copies[2 + e].wait()
        u = [mm(rows[e, at, :], gate_up(e, slice(ff, 2 * ff))) for at in blocks]
        copies[4 + e].wait()
        down_t = down[e].reshape(shards_of * part, ff)
        g = [mm(rows[2 + e, at, :], down_t) for at in blocks]
        for i, at in enumerate(blocks):
            sig = jax.nn.sigmoid(h[i])
            swished = h[i] * sig
            mixed[e, at, :] = (swished * u[i]).astype(BF)
            slope = sig * (1.0 + h[i] * (1.0 - sig))
            d_wide[e, at, 0:ff] = (g[i] * (u[i] * slope)).astype(BF)
            d_wide[e, at, ff : 2 * ff] = (g[i] * swished).astype(BF)
        store(e, mm_t(mixed[e], down_t))
        store(2 + e, mm_t(d_wide[e], gate_up(e, slice(0, 2 * ff))))
    row = lax.broadcasted_iota(jnp.int32, (1, CHUNK - LAST, 1), 1)
    rest = jnp.zeros((sources, CHUNK - LAST, width), F32)
    for kind in range(KINDS):
        rest = jnp.where(row == kind, last[kind], rest)
    back[:, LAST:CHUNK, :] = rest.astype(BF)


def stack_kernel(w_gate, w_up, w_down_t, out, sems):
    local = w_gate.shape[0]
    copies = [
        pltpu.make_async_copy(w, out.at[i * local : (i + 1) * local], sems.at[i])
        for i, w in enumerate((w_gate, w_up, w_down_t))
    ]
    for c in copies:
        c.start()
    for c in copies:
        c.wait()


def combine_kernel(
    back, mix, mix_last, hidden, inv, gain, grads, proj, out, feat_grad
):
    n, _, width = back.shape
    side = LAST // 2
    last = back[:, LAST:CHUNK, :].reshape(n * (CHUNK - LAST), width)

    def total_of(i):
        main = back[:, side * i : side * (i + 1), :].reshape(n * side, width)
        return mm(mix[i], main) + mm(mix_last[i], last)

    hf = hidden[...].astype(F32)
    out[...] = (hf + total_of(0)).astype(BF)
    scaled = total_of(1) * gain[...]
    scale = inv[...]
    centre = jnp.mean(hf * scaled, axis=1, keepdims=True)
    total = grads[...].astype(F32) + scale * scaled - hf * (scale * scale * scale) * centre
    feat_grad[...] = mm_t(total.astype(BF), proj[...]).astype(BF)


def shape(dims, dtype):
    return jax.ShapeDtypeStruct(dims, dtype)


def params(mib):
    return pltpu.CompilerParams(vmem_limit_bytes=mib * 1024 * 1024)


VMEM = pl.BlockSpec(memory_space=pltpu.VMEM)
HBM = pl.BlockSpec(memory_space=pltpu.HBM)


def shards(
    feats, proj, proj_bias, norm_gain, expert_ids, gate_codes, w_gate, w_up, w_down_t, out_grad
):
    toks, width = out_grad.shape
    sources = lax.axis_size("expert")
    local, part, ff = w_gate.shape
    bias, gain = proj_bias.reshape(1, width), norm_gain.reshape(1, width)
    stacked = pl.pallas_call(
        stack_kernel,
        out_shape=shape((3 * local, part, ff), BF),
        in_specs=[HBM] * 3,
        out_specs=HBM,
        scratch_shapes=[pltpu.SemaphoreType.DMA((3,))],
        compiler_params=params(16),
        name="stack",
    )(w_gate, w_up, w_down_t)
    weights = lax.all_gather(stacked, "dp", axis=0, tiled=False)

    send, hidden, inv, mix, mix_last = pl.pallas_call(
        prepare_kernel,
        out_shape=(
            shape((sources, CHUNK, width), BF),
            shape((toks, width), BF),
            shape((toks, 1), F32),
            shape((2, toks, sources * LAST // 2), BF),
            shape((2, toks, sources * (CHUNK - LAST)), BF),
        ),
        in_specs=[VMEM] * 7,
        out_specs=(VMEM,) * 5,
        compiler_params=params(28),
        name="prepare",
    )(feats, proj, bias, gain, expert_ids.T, gate_codes.T, out_grad)
    received = lax.all_to_all(send, "expert", split_axis=0, concat_axis=0, tiled=True)
    slots = sources * (MAIN + 1)
    rows = pl.pallas_call(
        arrange_kernel,
        out_shape=shape((KINDS, slots, width), BF),
        in_specs=[VMEM],
        out_specs=VMEM,
        compiler_params=params(28),
        name="arrange",
    )(received)
    results = pl.pallas_call(
        expert_kernel,
        out_shape=shape((sources, CHUNK, width), BF),
        in_specs=[VMEM, HBM],
        out_specs=VMEM,
        scratch_shapes=[
            pltpu.VMEM((local, weights.shape[0], part, 2 * ff), BF),
            pltpu.VMEM((local, weights.shape[0], part, ff), BF),
            pltpu.VMEM((local, slots, ff), BF),
            pltpu.VMEM((local, slots, 2 * ff), BF),
            pltpu.SemaphoreType.DMA((3 * local,)),
        ],
        compiler_params=params(46),
        name="experts",
    )(rows, weights)
    back = lax.all_to_all(results, "expert", split_axis=0, concat_axis=0, tiled=True)
    return pl.pallas_call(
        combine_kernel,
        out_shape=(shape((toks, width), BF), shape(feats.shape, BF)),
        in_specs=[VMEM] * 8,
        out_specs=(VMEM,) * 2,
        compiler_params=params(28),
        name="combine",
    )(back, mix, mix_last, hidden, inv, gain, out_grad, proj)


def solution(mesh):
    tokens = P(("dp", "expert"), None)
    experts = P("expert", "dp", None)
    in_specs = (tokens, P(), P(), P(), tokens, tokens, experts, experts, experts, tokens)
    return jax.shard_map(
        shards, mesh=mesh, in_specs=in_specs, out_specs=(tokens, tokens), check_vma=False
    )
```
